256 devices in a mesh: section: 2 (over core), dp: 8 (over y, z_lo), tensor: 16 (over x, z_hi).
Axes of the slice: x: 4, y: 4, z: 8 (z_hi: 4, z_lo: 2; z = z_hi * 2 + z_lo), core: 2. Of those that a mesh axis runs over, the one named last changes fastest.
Arguments:
- residual_parts: bfloat16 [2, 3072, 16384], P('section', 'dp', 'tensor'), may hold values from -120 to 120
- attn_out: bfloat16 [2, 3072, 16384], P('section', 'dp', 'tensor'), may hold values from -6 to 6
- ffn_input: bfloat16 [2, 3072, 53248], P('section', 'dp', 'tensor'), may hold values from -6 to 6
- norm_gain: float32 [2, 16384], P('section', 'tensor'), may hold values from 0.25 to 1.75
- mixing: bfloat16 [2, 52, 52], P('section'), may hold values from -0.875 to 0.875
- blocks: int32 [2, 2], P('section'), may hold values from 0 to 25, as said below
Outputs:
- hess_in: float32 [2, 16384, 1024], P('section', 'tensor', 'dp')
- hess_o: float32 [2, 16384, 1024], P('section', 'tensor', 'dp')
- hess_down: float32 [2, 2048, 2048], P('section', 'tensor', 'dp')
The draws below stay inside these ranges and needn't reach their ends.
Inputs may be any that keep to these rules, and one draw needn't show every extreme that they name: `blocks`: entry [s, 0] is below 16; entry [s, 1] is below 26. In every draw one layer has entry [s, 0] = 0 and entry [s, 1] = 25.
All inputs are finite; a program needn't handle non-finite values.
Results may differ from the reference program's by a relative error of at most 0.0038.
Values may be sent and summed in bfloat16 or wider, within the bound.
No kernel may reach another device: no remote copies, remote signals or barrier semaphores. Data moves between devices by JAX's collectives and lax.ppermute only.
A program may use at most 64 MiB of HBM per device.

```python
import math
import jax
import jax.numpy as jnp
from jax import lax

D = 16384
FF = 53248
KB = 52
HBLK = 1024
BLK = 2048
MB_TOK = 192
KA = 1024
TOKENS = 3072
N_SECTION = 2


def draw_residual_parts(key, part):
    key_base, key_rows, key_cols, key_delta = jax.random.split(jax.random.fold_in(key, 11), 4)
    base = jax.random.normal(key_base, (TOKENS, D), jnp.float32)
    row_scale = jnp.exp(jax.random.uniform(key_rows, (TOKENS,), jnp.float32, 0.0, math.log(10.0)))
    rising = jnp.exp(math.log(3.0) * jnp.arange(D, dtype=jnp.float32) / D)
    col_scale = rising * jnp.exp(jax.random.uniform(key_cols, (D,), jnp.float32, 0.0, math.log(10.0))) / 3.0
    stream = base * row_scale[:, None] * col_scale[None, :]
    update = 2.0 * jax.random.normal(key_delta, (TOKENS, D), jnp.float32) * row_scale[:, None]
    parts = jnp.stack([stream, update] + [update] * (N_SECTION - 2))
    return jnp.clip(parts, -120.0, 120.0).astype(jnp.bfloat16)


def draw_blocks(key, part):
    key_in, key_down, key_pick = jax.random.split(jax.random.fold_in(key, 23), 3)
    first = jax.random.randint(key_in, (N_SECTION,), 0, D // HBLK, jnp.int32)
    second = jax.random.randint(key_down, (N_SECTION,), 0, FF // BLK, jnp.int32)
    picked = jax.random.randint(key_pick, (), 0, N_SECTION, jnp.int32)
    is_picked = jnp.arange(N_SECTION, dtype=jnp.int32) == picked
    first = jnp.where(is_picked, 0, first).astype(jnp.int32)
    second = jnp.where(is_picked, FF // BLK - 1, second).astype(jnp.int32)
    return jnp.stack([first, second], axis=1)


def levels(stream_key, dims, pieces, least, high):
    loudness = 1.0
    for dim, blocks in pieces:
        steps = jax.random.uniform(jax.random.fold_in(jax.random.fold_in(stream_key, 6), dim), (blocks,), jnp.float32, least / len(pieces), high / len(pieces))
        loudness = loudness * jnp.repeat(jnp.exp(steps), dims[dim] // blocks).reshape((-1,) + (1,) * (len(dims) - 1 - dim))
    return loudness


def normal_values(stream_key, shape, spread, limit, cuts=(), kind=jnp.bfloat16):
    drawn = spread * jax.random.normal(stream_key, shape, jnp.float32)
    if cuts:
        drawn = drawn * levels(stream_key, shape, cuts, -0.22, 0.18)
    return jnp.clip(drawn, -limit, limit).astype(kind)


def setup_inputs(seed: int = 0) -> dict:
    key_list = jax.random.split(jax.random.key(seed), 7)
    residual_parts = draw_residual_parts(jax.random.fold_in(key_list[6], 71), 0)
    attn_out = normal_values(key_list[1], (N_SECTION, TOKENS, D), 1.0, 6.0, ((0, 2), (1, 8), (2, 16)))
    ffn_input = normal_values(key_list[2], (N_SECTION, TOKENS, FF), 1.0, 6.0, ((0, 2), (1, 8), (2, 16)))
    norm_gain = jnp.clip(1.0 + 0.15 * jax.random.normal(key_list[3], (N_SECTION, D), jnp.float32), 0.25, 1.75)
    mixing = normal_values(key_list[4], (N_SECTION, KB, KB), KB ** -0.5, 0.875, ((0, 2),))
    blocks = draw_blocks(jax.random.fold_in(key_list[6], 71), 0)
    return {"residual_parts": residual_parts, "attn_out": attn_out, "ffn_input": ffn_input, "norm_gain": norm_gain, "mixing": mixing, "blocks": blocks}


EPS = 1e-05

def bit_parity(values):
    total = jnp.zeros_like(values)
    for position in range(16):
        total = total + values // (1 << position) % 2
    return total % 2

def sylvester(order):
    index = jnp.arange(order, dtype=jnp.int32)
    parity = bit_parity(jnp.bitwise_and(index[:, None], index[None, :]))
    return (1 - 2 * parity).astype(jnp.float32)

def gram(left, right):
    return jnp.dot(left.T, right, preferred_element_type=jnp.float32)

def down_block(hidden, mixing_one, start):
    width_a = BLK // KB + 2
    first_a = jnp.minimum(start // KB, KA - width_a).astype(jnp.int32)
    chosen = lax.dynamic_slice_in_dim(sylvester(KA), first_a, width_a, 1)
    inner = (start - first_a * KB).astype(jnp.int32)
    factor = mixing_one.astype(jnp.float32)

    def one_block(token_rows):
        cube = token_rows.astype(jnp.float32).reshape(MB_TOK, KA, KB)
        mixed = jnp.einsum('rak,kc->rac', cube, factor, precision=lax.Precision.HIGHEST)
        turned = jnp.einsum('rac,ae->rec', mixed, chosen, precision=lax.Precision.HIGHEST)
        turned = turned / math.sqrt(KA)
        flat = turned.reshape(MB_TOK, width_a * KB)
        return lax.dynamic_slice_in_dim(flat, inner, BLK, 1).astype(jnp.bfloat16)
    grouped = hidden.reshape(TOKENS // MB_TOK, MB_TOK, FF)
    return lax.map(one_block, grouped).reshape(TOKENS, BLK)

def reference(residual_parts, attn_out, ffn_input, norm_gain, mixing, blocks):
    scale = 2.0 / TOKENS
    list_in, list_o, list_down = ([], [], [])
    for layer in range(N_SECTION):
        layer_in = residual_parts[layer].astype(jnp.float32)
        if layer > 0:
            layer_in = residual_parts[layer - 1].astype(jnp.float32) + layer_in
        mean_sq = lax.optimization_barrier(jnp.mean(layer_in * layer_in, axis=1))
        normed = (layer_in * lax.rsqrt(mean_sq + EPS)[:, None] * norm_gain[layer][None, :]).astype(jnp.bfloat16)
        first = (blocks[layer, 0] * HBLK).astype(jnp.int32)
        norm_cols = lax.dynamic_slice_in_dim(normed, first, HBLK, 1)
        list_in.append(scale * gram(normed, norm_cols))
        attention = attn_out[layer]
        attn_cols = lax.dynamic_slice_in_dim(attention, first, HBLK, 1)
        list_o.append(scale * gram(attention, attn_cols))
        start = (blocks[layer, 1] * BLK).astype(jnp.int32)
        down_cols = down_block(ffn_input[layer], mixing[layer], start)
        list_down.append(scale * gram(down_cols, down_cols))
    return (jnp.stack(list_in), jnp.stack(list_o), jnp.stack(list_down))
```

```python
import functools
import math

import jax
import jax.numpy as jnp
from jax import lax
from jax.experimental import pallas as pl
from jax.experimental.pallas import tpu as pltpu
from jax.sharding import Mesh
from jax.sharding import PartitionSpec as P

D = 16384
KB = 52
HBLK = 1024
BLK = 2048
EPS = 1e-05
N = 4
BF = jnp.bfloat16
F32 = jnp.float32


def back(x, axis, k):
    return lax.ppermute(x, axis, [(i, (i - k) % N) for i in range(N)])


def swap(x, axis):
    return lax.ppermute(x, axis, [(0, 1), (1, 0)])


def choose(arrays, index):
    out = arrays[0]
    for i in range(1, len(arrays)):
        out = jnp.where(index == i, arrays[i], out)
    return out


def gram(left, right):
    return lax.dot_general(
        left, right, (((0,), (0,)), ((), ())), preferred_element_type=F32
    )


def rotate_kernel(scal, x_ref, mix_ref, o_ref, w_ref, acc_ref):
    rows, width = x_ref.shape[1], x_ref.shape[2]
    cols = o_ref.shape[1]
    start, member = scal[0], scal[1]
    group = mix_ref.shape[0]
    j = lax.broadcasted_iota(jnp.int32, (8, cols), 1)[:1] + start
    a = jnp.floor((j.astype(F32) + 0.5) * (1.0 / KB)).astype(jnp.int32)
    c = j - a * KB
    high = jnp.bitwise_and(a // 64, member)
    parity = high
    for s in (1, 2, 3):
        parity = jnp.bitwise_xor(parity, lax.shift_right_logical(high, s))
    parity = jnp.bitwise_and(parity, 1)
    scale = (1.0 - 2.0 * parity.astype(F32)) / 32.0
    hot = jnp.where(
        lax.broadcasted_iota(jnp.int32, (KB, cols), 0) == c, 1.0, 0.0
    ).astype(BF)
    base = jnp.dot(mix_ref[...], hot, preferred_element_type=F32)
    row = lax.broadcasted_iota(jnp.int32, (group, 1), 0)
    q = (
        (row >= KB).astype(jnp.int32)
        + (row >= 2 * KB).astype(jnp.int32)
        + (row >= 3 * KB).astype(jnp.int32)
    )
    both = jnp.bitwise_and(q, jnp.bitwise_and(a, 3))
    odd = jnp.bitwise_and(jnp.bitwise_xor(both, lax.shift_right_logical(both, 1)), 1)
    base = (base * (scale * (1.0 - 2.0 * odd.astype(F32)))).astype(BF)
    for g in range(width // group):
        bits = jnp.bitwise_and(lax.shift_right_logical(a, 2), g)
        for s in (2, 1):
            bits = jnp.bitwise_xor(bits, lax.shift_right_logical(bits, s))
        sign = (1.0 - 2.0 * jnp.bitwise_and(bits, 1).astype(F32)).astype(BF)
        w_ref[g * group : (g + 1) * group, :] = base * sign
    step = 256
    acc_ref[...] = jnp.zeros_like(acc_ref)

    def body(i, carry):
        at = pl.multiple_of(i * step, step)
        acc_ref[...] += jnp.dot(
            x_ref[0, :, pl.ds(at, step)],
            w_ref[pl.ds(at, step), :],
            preferred_element_type=F32,
        )
        return carry

    lax.fori_loop(0, width // step, body, 0)
    o_ref[...] = acc_ref[...].astype(o_ref.dtype)


def rotate(ffn, mix4, start, member, cols, dtype):
    rows, width = ffn.shape[1], ffn.shape[2]
    scal = jnp.stack([start, member]).astype(jnp.int32)
    return pl.pallas_call(
        rotate_kernel,
        out_shape=jax.ShapeDtypeStruct((rows, cols), dtype),
        grid_spec=pltpu.PrefetchScalarGridSpec(
            num_scalar_prefetch=1,
            grid=(1,),
            in_specs=[
                pl.BlockSpec(ffn.shape, lambda i, s: (0, 0, 0)),
                pl.BlockSpec(mix4.shape, lambda i, s: (0, 0)),
            ],
            out_specs=pl.BlockSpec((rows, cols), lambda i, s: (0, 0)),
            scratch_shapes=[
                pltpu.VMEM((width, cols), BF),
                pltpu.VMEM((rows, cols), F32),
            ],
        ),
        compiler_params=pltpu.CompilerParams(vmem_limit_bytes=24 * 1024 * 1024),
        cost_estimate=pl.CostEstimate(
            flops=2 * rows * width * cols,
            bytes_accessed=2 * rows * width + 2 * rows * cols,
            transcendentals=0,
        ),
    )(scal, ffn, mix4)


def spread(block, own_x, own_z, x, z):
    rows, cols = block.shape
    w = cols // N

    def quarter(at):
        return lax.dynamic_slice_in_dim(block, at * w, w, 1)

    got = [quarter(x)] + [back(quarter((x - k) % N), "x", k) for k in range(1, N)]
    mine = choose(got, (own_x - x) % N)
    over_z = [mine] + [back(mine, "zh", k) for k in range(1, N)]
    piece = choose(over_z, (own_z - z) % N)
    return [piece] + [back(piece, "x", k) for k in range(1, N)]


def to_columns(left, quarters, x, y, zl):
    def part(dest):
        return gram(left, choose(quarters, (dest - x) % N))

    total = part(y)
    for k in range(1, N):
        total = total + back(part((y - k) % N).astype(BF), "y", k).astype(F32)
    w = total.shape[1] // 2
    low, high = total[:, :w], total[:, w:]
    keep = jnp.where(zl == 0, low, high)
    give = jnp.where(zl == 0, high, low)
    return keep + swap(give, "zl")


def local(residual_parts, attn_out, ffn_input, norm_gain, mixing, blocks):
    local_f = ffn_input.shape[2]
    token_rows = residual_parts.shape[1]
    tokens = token_rows * lax.axis_size("y") * lax.axis_size("zl")
    x, z = lax.axis_index("x"), lax.axis_index("zh")
    y, zl = lax.axis_index("y"), lax.axis_index("zl")
    member = x * N + z
    first, second = blocks[0, 0], blocks[0, 1]
    own_x, own_z = first // N, first % N

    own_part = residual_parts[0]
    earlier = lax.ppermute(own_part, "section", [(0, 1)])
    attention = attn_out[0]

    layer_in = earlier.astype(F32) + own_part.astype(F32)
    squares = jnp.sum(layer_in * layer_in, axis=1)
    for axis in ("x", "zh"):
        squares = squares + sum(back(squares, axis, k) for k in range(1, N))
    normed = (
        layer_in * lax.rsqrt(squares / D + EPS)[:, None] * norm_gain[0][None, :]
    ).astype(BF)

    attn_quarters = spread(attention, own_x, own_z, x, z)
    norm_quarters = spread(normed, own_x, own_z, x, z)

    mix4 = jnp.tile(mixing[0], (4, 1))
    start = second * BLK
    wide = BLK // N
    sent = [
        back(
            rotate(ffn_input, mix4, start + ((x - k) % N) * wide, member, wide, BF),
            "x",
            k,
        )
        for k in range(1, N)
    ]
    own = rotate(ffn_input, mix4, start + x * wide, member, wide, F32)
    over_x = own
    for s in sent:
        over_x = over_x + s.astype(F32)
    slim = wide // N

    def strip(at):
        return lax.dynamic_slice_in_dim(over_x, at * slim, slim, 1)

    cols = strip(z)
    for k in range(1, N):
        cols = cols + back(strip((z - k) % N).astype(BF), "zh", k).astype(F32)
    cols = cols.astype(BF)
    row_block = jnp.concatenate(
        [cols] + [back(cols, "zh", k) for k in range(1, N)], axis=1
    )
    all_blocks = [row_block] + [back(row_block, "x", k) for k in range(1, N)]

    scale = 2.0 / tokens
    hess_o = to_columns(attention, attn_quarters, x, y, zl)
    hess_in = to_columns(normed, norm_quarters, x, y, zl)

    def down_part(dest):
        return gram(cols, choose(all_blocks, (dest - x) % N))

    down = down_part(y)
    for k in range(1, N):
        down = down + back(down_part((y - k) % N).astype(BF), "y", k).astype(F32)

    def half(which):
        pieces = [down[:, i * slim : (i + 1) * slim] for i in range(N)]
        return jnp.concatenate(
            [choose(pieces, (2 * which + i - z) % N) for i in range(2)], axis=1
        )

    down = half(zl) + swap(half(1 - zl), "zl")
    return ((scale * hess_in)[None], (scale * hess_o)[None], (scale * down)[None])


def solution(mesh):
    finer = Mesh(
        mesh.devices.reshape(mesh.shape["section"], 4, 2, 4, 4),
        ("section", "y", "zl", "x", "zh"),
    )
    dp, tensor = ("y", "zl"), ("x", "zh")
    in_specs = (
        P("section", dp, tensor),
        P("section", dp, tensor),
        P("section", dp, tensor),
        P("section", tensor),
        P("section", None, None),
        P("section", None),
    )
    out_specs = (P("section", tensor, dp),) * 3
    return jax.shard_map(local, mesh=finer, in_specs=in_specs, out_specs=out_specs, check_vma=False)
```

```python
import math

import jax
import jax.numpy as jnp
from jax import lax
from jax.experimental import pallas as pl
from jax.experimental.pallas import tpu as pltpu
from jax.sharding import Mesh
from jax.sharding import PartitionSpec as P

D = 16384
KB = 52
HBLK = 1024
BLK = 2048
EPS = 1e-05
N = 4
BF = jnp.bfloat16
F32 = jnp.float32
FLIP_U = [(0, 1), (1, 0), (2, 3), (3, 2)]
FLIP_V = [(0, 3), (3, 0), (1, 2), (2, 1)]


class Ring:
    def __init__(self, axis, first="u"):
        self.axis, self.first = axis, first
        i = lax.axis_index(axis)
        self.index = i
        self.a, self.b = self.coords(i)
        self.flip = (FLIP_U, FLIP_V) if first == "u" else (FLIP_V, FLIP_U)

    def coords(self, i):
        v = i // 2
        u = jnp.bitwise_xor(i % 2, v)
        return (u, v) if self.first == "u" else (v, u)

    def place(self, a, b):
        u, v = (a, b) if self.first == "u" else (b, a)
        return 2 * v + jnp.bitwise_xor(u, v)

    def send(self, x, step):
        return lax.ppermute(x, self.axis, self.flip[step])

    def relative(self, i):
        a, b = self.coords(i)
        return jnp.bitwise_xor(a, self.a) + 2 * jnp.bitwise_xor(b, self.b)

    def fold(self, get, width, combine_a, combine_b, wire):
        a, b = self.a, self.b
        give = get([self.place(1 - a, b), self.place(1 - a, 1 - b)]).astype(wire)
        came = self.send(give, 0)
        half = combine_a(get([self.place(a, b), self.place(a, 1 - b)]), came)
        mine, other = half[:, :width], half[:, width:]
        return combine_b(mine, self.send(other.astype(wire), 1))

    def reduce(self, get, width, wire=BF):
        def add(x, y):
            return x + y.astype(F32)

        return self.fold(get, width, add, add, wire)

    def pick_piece(self, get, width, owner):
        oa, ob = self.coords(owner)
        return self.fold(
            get,
            width,
            lambda x, y: jnp.where(oa == self.a, x, y),
            lambda x, y: jnp.where(ob == self.b, x, y),
            BF,
        )

    def pick(self, x, owner):
        oa, ob = self.coords(owner)
        x = jnp.where(oa == self.a, x, self.send(x, 0))
        return jnp.where(ob == self.b, x, self.send(x, 1))

    def total(self, x):
        x = x + self.send(x, 0)
        return x + self.send(x, 1)

    def gather(self, x):
        one = self.send(x, 0)
        two = self.send(jnp.concatenate([x, one], axis=1), 1)
        w = x.shape[1]
        return [x, one, two[:, :w], two[:, w:]]


def swap(x, axis):
    return lax.ppermute(x, axis, [(0, 1), (1, 0)])


def choose(arrays, index):
    out = arrays[0]
    for i in range(1, len(arrays)):
        out = jnp.where(index == i, arrays[i], out)
    return out


def side_by_side(arrays):
    return jnp.concatenate(arrays, axis=1)


def after(x, *others):
    return lax.optimization_barrier((x, *others))[0]


def gram(left, right):
    return lax.dot_general(
        left, right, (((0,), (0,)), ((), ())), preferred_element_type=F32
    )


def rotate_kernel(scal, x_ref, mix_ref, o_ref, w_ref):
    width = x_ref.shape[2]
    cols = o_ref.shape[1]
    member = scal[2]
    group = mix_ref.shape[0]
    lane = lax.broadcasted_iota(jnp.int32, (8, cols), 1)[:1]
    half = cols // 2
    j = jnp.where(lane < half, scal[0] + lane, scal[1] + lane - half)
    a = jnp.floor((j.astype(F32) + 0.5) * (1.0 / KB)).astype(jnp.int32)
    c = j - a * KB
    high = jnp.bitwise_and(a // 64, member)
    parity = high
    for s in (1, 2, 3):
        parity = jnp.bitwise_xor(parity, lax.shift_right_logical(high, s))
    parity = jnp.bitwise_and(parity, 1)
    scale = (1.0 - 2.0 * parity.astype(F32)) / 32.0
    hot = jnp.where(
        lax.broadcasted_iota(jnp.int32, (KB, cols), 0) == c, 1.0, 0.0
    ).astype(BF)
    base = jnp.dot(mix_ref[...], hot, preferred_element_type=F32)
    row = lax.broadcasted_iota(jnp.int32, (group, 1), 0)
    q = (
        (row >= KB).astype(jnp.int32)
        + (row >= 2 * KB).astype(jnp.int32)
        + (row >= 3 * KB).astype(jnp.int32)
    )
    both = jnp.bitwise_and(q, jnp.bitwise_and(a, 3))
    odd = jnp.bitwise_and(jnp.bitwise_xor(both, lax.shift_right_logical(both, 1)), 1)
    base = (base * (scale * (1.0 - 2.0 * odd.astype(F32)))).astype(BF)
    for g in range(width // group):
        bits = jnp.bitwise_and(lax.shift_right_logical(a, 2), g)
        for s in (2, 1):
            bits = jnp.bitwise_xor(bits, lax.shift_right_logical(bits, s))
        sign = (1.0 - 2.0 * jnp.bitwise_and(bits, 1).astype(F32)).astype(BF)
        w_ref[g * group : (g + 1) * group, :] = base * sign
    o_ref[...] = jnp.dot(
        x_ref[0], w_ref[...], preferred_element_type=F32
    ).astype(o_ref.dtype)


def rotate(ffn, mix4, scal, cols, dtype):
    rows, width = ffn.shape[1], ffn.shape[2]
    return pl.pallas_call(
        rotate_kernel,
        out_shape=jax.ShapeDtypeStruct((rows, cols), dtype),
        grid_spec=pltpu.PrefetchScalarGridSpec(
            num_scalar_prefetch=1,
            grid=(1,),
            in_specs=[
                pl.BlockSpec(ffn.shape, lambda i, s: (0, 0, 0)),
                pl.BlockSpec(mix4.shape, lambda i, s: (0, 0)),
            ],
            out_specs=pl.BlockSpec((rows, cols), lambda i, s: (0, 0)),
            scratch_shapes=[pltpu.VMEM((width, cols), BF)],
        ),
        compiler_params=pltpu.CompilerParams(vmem_limit_bytes=24 * 1024 * 1024),
        cost_estimate=pl.CostEstimate(
            flops=2 * rows * width * cols,
            bytes_accessed=2 * rows * width + 2 * rows * cols,
            transcendentals=0,
        ),
    )(scal, ffn, mix4)


def spread(block, own_x, own_z, first):
    rx, rz = Ring("x", first), Ring("zh", first)
    w = block.shape[1] // N

    def get(places):
        return side_by_side(
            [lax.dynamic_slice_in_dim(block, p * w, w, 1) for p in places]
        )

    piece = rz.pick(rx.pick_piece(get, w, own_x), own_z)
    return rx.gather(piece), rx


def to_columns(left, quarters, rx, zl):
    w = quarters[0].shape[1]
    rows = left.shape[1] // 2
    sums = []
    for part, first in enumerate(("u", "v")):
        strip = left[:, part * rows : (part + 1) * rows]

        def get(places):
            return gram(
                strip, side_by_side([choose(quarters, rx.relative(p)) for p in places])
            )

        sums.append(Ring("y", first).reduce(get, w))
    total = jnp.concatenate(sums, axis=0)
    w = w // 2
    low, high = total[:, :w], total[:, w:]
    keep = jnp.where(zl == 0, low, high)
    give = jnp.where(zl == 0, high, low)
    return keep + swap(give.astype(BF), "zl").astype(F32)


def local(residual_parts, attn_out, ffn_input, norm_gain, mixing, blocks):
    token_rows = residual_parts.shape[1]
    tokens = token_rows * lax.axis_size("y") * lax.axis_size("zl")
    zl = lax.axis_index("zl")
    member = lax.axis_index("x") * N + lax.axis_index("zh")
    own_x, own_z = blocks[0, 0] // N, blocks[0, 0] % N
    start = blocks[0, 1] * BLK

    own_part = residual_parts[0]
    earlier = lax.ppermute(own_part, "section", [(0, 1)])
    attention = attn_out[0]

    layer_in = earlier.astype(F32) + own_part.astype(F32)
    squares = jnp.sum(layer_in * layer_in, axis=1)
    start = after(start, squares)
    squares = Ring("zh").total(Ring("x").total(squares))
    normed = (
        layer_in * lax.rsqrt(squares / D + EPS)[:, None] * norm_gain[0][None, :]
    ).astype(BF)

    attn_quarters, attn_ring = spread(attention, own_x, own_z, "v")
    norm_quarters, norm_ring = spread(normed, own_x, own_z, "u")

    mix4 = jnp.tile(mixing[0], (4, 1))
    wide = BLK // N
    sub = wide // 2
    pieces = []
    for part, first in enumerate(("u", "v")):
        ring = Ring("x", first)

        def get(places, dtype, part=part):
            scal = [start + p * wide + part * sub for p in places] + [member]
            return rotate(ffn_input, mix4, jnp.stack(scal), 2 * sub, dtype)

        give = get([ring.place(1 - ring.a, ring.b), ring.place(1 - ring.a, 1 - ring.b)], BF)
        pieces.append((ring, get, ring.send(give, 0)))
    summed = []
    for ring, get, came in pieces:
        kept = get([ring.place(ring.a, ring.b), ring.place(ring.a, 1 - ring.b)], F32)
        half = kept + came.astype(F32)
        summed.append(
            half[:, :sub] + ring.send(half[:, sub:].astype(BF), 1).astype(F32)
        )
    over_x = side_by_side(summed)
    slim = wide // N
    rows = token_rows // 2
    cols = []
    for part, first in enumerate(("u", "v")):
        strip = over_x[part * rows : (part + 1) * rows]
        strips = [strip[:, i * slim : (i + 1) * slim] for i in range(N)]

        def get(places, strips=strips):
            return side_by_side([choose(strips, p) for p in places])

        cols.append(Ring("zh", first).reduce(get, slim).astype(BF))
    cols = jnp.concatenate(cols, axis=0)
    rz = Ring("zh")
    row_block = side_by_side(rz.gather(cols))
    rx = Ring("x")
    all_blocks = rx.gather(row_block)

    scale = 2.0 / tokens
    hess_o = to_columns(attention, attn_quarters, attn_ring, zl)
    hess_in = to_columns(normed, norm_quarters, norm_ring, zl)

    def down_get(places):
        return gram(cols, side_by_side([choose(all_blocks, rx.relative(p)) for p in places]))

    down = Ring("y").reduce(down_get, wide)
    pieces = [down[:, i * slim : (i + 1) * slim] for i in range(N)]

    def half(which):
        return side_by_side(
            [choose(pieces, rz.relative(2 * which + i)) for i in range(2)]
        )

    down = half(zl) + swap(half(1 - zl), "zl")
    return ((scale * hess_in)[None], (scale * hess_o)[None], (scale * down)[None])


def solution(mesh):
    finer = Mesh(
        mesh.devices.reshape(mesh.shape["section"], 4, 2, 4, 4),
        ("section", "y", "zl", "x", "zh"),
    )
    dp, tensor = ("y", "zl"), ("x", "zh")
    in_specs = (
        P("section", dp, tensor),
        P("section", dp, tensor),
        P("section", dp, tensor),
        P("section", tensor),
        P("section", None, None),
        P("section", None),
    )
    out_specs = (P("section", tensor, dp),) * 3
    return jax.shard_map(local, mesh=finer, in_specs=in_specs, out_specs=out_specs, check_vma=False)
```

```python
import math

import jax
import jax.numpy as jnp
from jax import lax
from jax.experimental import pallas as pl
from jax.experimental.pallas import tpu as pltpu
from jax.sharding import Mesh
from jax.sharding import PartitionSpec as P

D = 16384
KB = 52
HBLK = 1024
BLK = 2048
EPS = 1e-05
N = 4
BF = jnp.bfloat16
F32 = jnp.float32
FLIP_U = [(0, 1), (1, 0), (2, 3), (3, 2)]
FLIP_V = [(0, 3), (3, 0), (1, 2), (2, 1)]


class Ring:
    def __init__(self, axis, first="u", name="r"):
        self.axis, self.first, self.name = axis, first, name
        i = lax.axis_index(axis)
        self.a, self.b = self.coords(i)
        self.flip = (FLIP_U, FLIP_V) if first == "u" else (FLIP_V, FLIP_U)

    def coords(self, i):
        v = i // 2
        u = jnp.bitwise_xor(i % 2, v)
        return (u, v) if self.first == "u" else (v, u)

    def place(self, a, b):
        u, v = (a, b) if self.first == "u" else (b, a)
        return 2 * v + jnp.bitwise_xor(u, v)

    def given(self):
        return [self.place(1 - self.a, self.b), self.place(1 - self.a, 1 - self.b)]

    def kept(self):
        return [self.place(self.a, self.b), self.place(self.a, 1 - self.b)]

    def send(self, x, step):
        with jax.named_scope(f"{self.name}_{self.axis}{step}"):
            return lax.ppermute(x, self.axis, self.flip[step])

    def relative(self, i):
        a, b = self.coords(i)
        return jnp.bitwise_xor(a, self.a) + 2 * jnp.bitwise_xor(b, self.b)

    def add(self, kept, came, width, axis, wire=BF):
        half = kept + came.astype(F32)
        mine = lax.slice_in_dim(half, 0, width, axis=axis)
        other = lax.slice_in_dim(half, width, 2 * width, axis=axis)
        return mine, self.send(other.astype(wire), 1)

    def reduce(self, get, width, axis=1, wire=BF):
        came = self.send(get(self.given()).astype(wire), 0)
        mine, last = self.add(get(self.kept()), came, width, axis, wire)
        return mine + last.astype(F32)

    def pick_piece(self, get, width, owner, line):
        oa, ob = self.coords(owner)
        came = self.send(line(get(self.given())), 0)
        yield
        half = jnp.where(oa == self.a, get(self.kept()), line.tie(came))
        mine, other = half[:, :width], half[:, width:]
        came = self.send(line(other), 1)
        yield
        yield jnp.where(ob == self.b, mine, line.tie(came))

    def total(self, x):
        x = x + self.send(x, 0)
        return x + self.send(x, 1)

    def gather(self, x):
        one = self.send(x, 0)
        two = self.send(jnp.concatenate([x, one], axis=1), 1)
        w = x.shape[1]
        return [x, one, two[:, :w], two[:, w:]]


class Line:
    def __init__(self):
        self.last = None

    def __call__(self, x):
        x = self.tie(x)
        self.last = x
        return x

    def tie(self, x):
        return x if self.last is None else lax.optimization_barrier((x, self.last))[0]


def swap(x, axis, name="s"):
    with jax.named_scope(f"{name}_{axis}"):
        return lax.ppermute(x, axis, [(0, 1), (1, 0)])


def choose(arrays, index):
    out = arrays[0]
    for i in range(1, len(arrays)):
        out = jnp.where(index == i, arrays[i], out)
    return out


def side_by_side(arrays):
    return jnp.concatenate(arrays, axis=1)


def after(x, *others):
    return lax.optimization_barrier((x, *others))[0]


def gram(left, right):
    return lax.dot_general(
        left, right, (((0,), (0,)), ((), ())), preferred_element_type=F32
    )


def rotate_kernel(scal, x_ref, mix_ref, o_ref, w_ref):
    width = x_ref.shape[2]
    cols = o_ref.shape[1]
    member = scal[2]
    group = mix_ref.shape[0]
    lane = lax.broadcasted_iota(jnp.int32, (8, cols), 1)[:1]
    half = cols // 2
    base_col = jnp.where(lane < half, scal[0], scal[1])
    z = jnp.bitwise_and(lax.shift_right_logical(lane, 7), half // 128 - 1)
    h = jnp.bitwise_and(lax.shift_right_logical(lane, 6), 1)
    j = base_col + h * half + z * 64 + jnp.bitwise_and(lane, 63)
    a = jnp.floor((j.astype(F32) + 0.5) * (1.0 / KB)).astype(jnp.int32)
    c = j - a * KB
    high = jnp.bitwise_and(a // 64, member)
    parity = high
    for s in (1, 2, 3):
        parity = jnp.bitwise_xor(parity, lax.shift_right_logical(high, s))
    parity = jnp.bitwise_and(parity, 1)
    scale = (1.0 - 2.0 * parity.astype(F32)) / 32.0
    hot = jnp.where(
        lax.broadcasted_iota(jnp.int32, (KB, cols), 0) == c, 1.0, 0.0
    ).astype(BF)
    base = jnp.dot(mix_ref[...], hot, preferred_element_type=F32)
    row = lax.broadcasted_iota(jnp.int32, (group, 1), 0)
    q = (
        (row >= KB).astype(jnp.int32)
        + (row >= 2 * KB).astype(jnp.int32)
        + (row >= 3 * KB).astype(jnp.int32)
    )
    both = jnp.bitwise_and(q, jnp.bitwise_and(a, 3))
    odd = jnp.bitwise_and(jnp.bitwise_xor(both, lax.shift_right_logical(both, 1)), 1)
    base = (base * (scale * (1.0 - 2.0 * odd.astype(F32)))).astype(BF)
    for g in range(width // group):
        bits = jnp.bitwise_and(lax.shift_right_logical(a, 2), g)
        for s in (2, 1):
            bits = jnp.bitwise_xor(bits, lax.shift_right_logical(bits, s))
        sign = (1.0 - 2.0 * jnp.bitwise_and(bits, 1).astype(F32)).astype(BF)
        w_ref[g * group : (g + 1) * group, :] = base * sign
    o_ref[...] = jnp.dot(
        x_ref[0], w_ref[...], preferred_element_type=F32
    ).astype(o_ref.dtype)


def rotate(ffn, mix4, scal, cols, dtype):
    rows, width = ffn.shape[1], ffn.shape[2]
    return pl.pallas_call(
        rotate_kernel,
        out_shape=jax.ShapeDtypeStruct((rows, cols), dtype),
        grid_spec=pltpu.PrefetchScalarGridSpec(
            num_scalar_prefetch=1,
            grid=(1,),
            in_specs=[
                pl.BlockSpec(ffn.shape, lambda i, s: (0, 0, 0)),
                pl.BlockSpec(mix4.shape, lambda i, s: (0, 0)),
            ],
            out_specs=pl.BlockSpec((rows, cols), lambda i, s: (0, 0)),
            scratch_shapes=[pltpu.VMEM((width, cols), BF)],
        ),
        compiler_params=pltpu.CompilerParams(vmem_limit_bytes=24 * 1024 * 1024),
        cost_estimate=pl.CostEstimate(
            flops=2 * rows * width * cols,
            bytes_accessed=2 * rows * width + 2 * rows * cols,
            transcendentals=0,
        ),
    )(scal, ffn, mix4)


def column_parts(left, quarters, rx, name, line):
    w = quarters[0].shape[1]
    rows = left.shape[1] // 2
    rings = [Ring("y", "u", name + "A"), Ring("y", "v", name + "B")]

    def get(part, places):
        right = side_by_side([choose(quarters, rx.relative(p)) for p in places])
        return gram(left[:, part * rows : (part + 1) * rows], right)

    came = [
        r.send(line(get(i, r.given()).astype(BF)), 0) for i, r in enumerate(rings)
    ]
    yield
    mine, last = [], []
    for i, r in enumerate(rings):
        half = get(i, r.kept()) + line.tie(came[i]).astype(F32)
        mine.append(half[:, :w])
        last.append(r.send(line(half[:, w:].astype(BF)), 1))
    yield
    yield jnp.concatenate(
        [m + line.tie(c).astype(F32) for m, c in zip(mine, last)], axis=0
    )


def local(residual_parts, attn_out, ffn_input, norm_gain, mixing, blocks):
    token_rows = residual_parts.shape[1]
    tokens = token_rows * lax.axis_size("y") * lax.axis_size("zl")
    zl = lax.axis_index("zl")
    member = lax.axis_index("x") * N + lax.axis_index("zh")
    own_x, own_z = blocks[0, 0] // N, blocks[0, 0] % N
    start = blocks[0, 1] * BLK
    line = Line()

    own_part = residual_parts[0]
    attention = attn_out[0]
    section = [(0, 1)]
    with jax.named_scope("sec0"):
        earlier = lax.ppermute(own_part, "section", section)
    own_raw = own_part
    next_part = swap(own_part, "zl", "raw")

    ax = Ring("x", "v", "O")
    aw = HBLK // N

    def attn_get(places):
        return side_by_side(
            [lax.dynamic_slice_in_dim(attention, p * aw, aw, 1) for p in places]
        )

    attn_steps = ax.pick_piece(attn_get, aw, own_x, line)
    next(attn_steps)

    layer_in = earlier.astype(F32) + own_raw.astype(F32)
    squares = line(jnp.sum(layer_in * layer_in, axis=1))
    qx, qz = Ring("x", "u", "q"), Ring("zh", "u", "q")
    q1 = qx.send(squares, 0)

    mix4 = jnp.tile(mixing[0], (4, 1))
    wide = BLK // N
    sub = wide // 2

    def rotated(part, places, dtype):
        scal = [start + p * wide + part * (sub // 2) for p in places] + [member]
        return line(rotate(ffn_input, mix4, line.tie(jnp.stack(scal)), 2 * sub, dtype))

    fr = [Ring("x", "u", "FA"), Ring("x", "v", "FB")]
    came = [fr[0].send(rotated(0, fr[0].given(), BF), 0)]
    squares = line(squares + line.tie(q1))
    q2 = qx.send(squares, 1)
    came.append(fr[1].send(rotated(1, fr[1].given(), BF), 0))
    squares = line(squares + line.tie(q2))
    q3 = qz.send(squares, 0)
    kept = [rotated(0, fr[0].kept(), F32)]
    next(attn_steps)
    squares = line(squares + line.tie(q3))
    q4 = qz.send(squares, 1)
    kept.append(rotated(1, fr[1].kept(), F32))
    squares = line(squares + line.tie(q4))
    next_squares = swap(squares, "zl", "q")
    with jax.named_scope("sec1"):
        next_earlier = lax.ppermute(line(next_part), "section", section)
    attn_piece = next(attn_steps)

    def normalize(part, before, total):
        total_in = before.astype(F32) + part.astype(F32)
        return (
            total_in * lax.rsqrt(total / D + EPS)[:, None] * norm_gain[0][None, :]
        ).astype(BF)

    normed = jnp.concatenate(
        [
            normalize(own_raw, earlier, squares),
            normalize(next_part, next_earlier, line.tie(next_squares)),
        ],
        axis=0,
    )
    normed = line(normed)
    nx = Ring("x", "u", "N")
    nw = aw // 2

    def norm_get(places):
        return side_by_side(
            [
                lax.dynamic_slice_in_dim(normed, p * aw + zl * nw, nw, 1)
                for p in places
            ]
        )

    norm_steps = nx.pick_piece(norm_get, nw, own_x, line)
    next(norm_steps)

    az = Ring("zh", "v", "O")
    oa, ob = az.coords(own_z)
    attn_far = az.send(line(attn_piece), 0)
    halves = [r.add(kept[i], line.tie(came[i]), sub, 1) for i, r in enumerate(fr)]
    attn_piece = jnp.where(oa == az.a, attn_piece, line.tie(attn_far))
    attn_far = az.send(line(attn_piece), 1)
    next(norm_steps)
    over_x = side_by_side([m + line.tie(c).astype(F32) for m, c in halves])
    slim = wide // N
    rows = token_rows // 2
    fz = [Ring("zh", "u", "FA"), Ring("zh", "v", "FB")]
    strips = [
        [over_x[i * rows : (i + 1) * rows, k * slim : (k + 1) * slim] for k in range(N)]
        for i in range(2)
    ]

    def strips_for(i, places):
        return side_by_side([choose(strips[i], p) for p in places])

    came = [
        r.send(line(strips_for(i, r.given()).astype(BF)), 0) for i, r in enumerate(fz)
    ]
    norm_piece = next(norm_steps)
    nz = Ring("zh", "u", "N")
    na, nb = nz.coords(own_z)
    norm_far = nz.send(line(norm_piece), 0)
    attn_piece = line(jnp.where(ob == az.b, attn_piece, line.tie(attn_far)))
    attn_one = ax.send(attn_piece, 0)
    mine, last = [], []
    for i, r in enumerate(fz):
        half = strips_for(i, r.kept()) + line.tie(came[i]).astype(F32)
        mine.append(half[:, :slim])
        last.append(r.send(line(half[:, slim:].astype(BF)), 1))
    norm_piece = jnp.where(na == nz.a, norm_piece, line.tie(norm_far))
    norm_far = nz.send(line(norm_piece), 1)
    attn_two = ax.send(line(side_by_side([attn_piece, line.tie(attn_one)])), 1)
    cols = jnp.concatenate(
        [(m + line.tie(c).astype(F32)).astype(BF) for m, c in zip(mine, last)], axis=0
    )
    cols = line(cols)
    rz, rx = Ring("zh", "u", "G"), Ring("x", "u", "G")
    z_one, x_one = rz.send(cols, 0), rx.send(cols, 0)
    norm_piece = line(jnp.where(nb == nz.b, norm_piece, line.tie(norm_far)))
    norm_one = nx.send(norm_piece, 0)
    norm_two = nx.send(line(side_by_side([norm_piece, line.tie(norm_one)])), 1)
    z_two = rz.send(line(side_by_side([cols, line.tie(z_one)])), 1)
    x_two = rx.send(line(side_by_side([cols, line.tie(x_one)])), 1)

    def split(x):
        w = x.shape[1] // 2
        return [x[:, :w], x[:, w:]]

    attn_quarters = [attn_piece, attn_one] + split(line.tie(attn_two))
    norm_quarters = [norm_piece, norm_one] + split(line.tie(norm_two))
    scale = 2.0 / tokens
    attn_parts = column_parts(attention, attn_quarters, ax, "O", line)
    next(attn_parts)
    norm_parts = column_parts(normed, norm_quarters, nx, "N", line)
    next(norm_parts)
    row_blocks = side_by_side([cols, z_one, line.tie(z_two)])
    col_blocks = [cols, x_one] + split(line.tie(x_two))
    def down_get(places):
        left = side_by_side([choose(col_blocks, rx.relative(p)) for p in places])
        return gram(left, row_blocks)

    fy = Ring("y", "u", "F")
    came = fy.send(line(down_get(fy.given()).astype(BF)), 0)
    next(attn_parts)
    half = down_get(fy.kept()) + line.tie(came).astype(F32)
    came = fy.send(line(half[slim:].astype(BF)), 1)
    next(norm_parts)
    total = next(attn_parts)
    low, high = total[:, : aw // 2], total[:, aw // 2 :]
    keep = jnp.where(zl == 0, low, high)
    give = jnp.where(zl == 0, high, low)
    attn_last = swap(line(give.astype(BF)), "zl", "O")
    down = half[:slim] + line.tie(came).astype(F32)
    n = slim // 2
    low, high = down[:n], down[n:]
    down = jnp.where(zl == 0, low, high) + swap(
        line(jnp.where(zl == 0, high, low)), "zl", "F"
    )
    hess_in = next(norm_parts)
    hess_o = keep + attn_last.astype(F32)
    chunks = [down[:, i * n : (i + 1) * n] for i in range(2 * N)]

    def rows_for(place):
        return side_by_side(
            [
                choose(chunks, 2 * rz.relative(2 * (place % 2) + e) + place // 2)
                for e in range(2)
            ]
        )

    give = jnp.concatenate([rows_for(p) for p in rz.given()], axis=0)
    came = rz.send(give, 0)
    last = rz.send(
        jnp.concatenate([rows_for(rz.kept()[1]), came[n:]], axis=0), 1
    )
    found = [rows_for(rz.kept()[0]), came[:n], last[:n], last[n:]]
    down = jnp.concatenate(
        [choose(found, rz.relative(i)) for i in range(N)], axis=0
    ).T
    return ((scale * hess_in)[None], (scale * hess_o)[None], (scale * down)[None])


def solution(mesh):
    finer = Mesh(
        mesh.devices.reshape(mesh.shape["section"], 4, 2, 4, 4),
        ("section", "y", "zl", "x", "zh"),
    )
    dp, tensor = ("y", "zl"), ("x", "zh")
    in_specs = (
        P("section", dp, tensor),
        P("section", dp, tensor),
        P("section", dp, tensor),
        P("section", tensor),
        P("section", None, None),
        P("section", None),
    )
    out_specs = (P("section", tensor, dp),) * 3
    return jax.shard_map(local, mesh=finer, in_specs=in_specs, out_specs=out_specs, check_vma=False)
```
